512 devices in a mesh: ctx: 64 (over z, x), ch: 8 (over y, core).
Axes of the slice: x: 4, y: 4, z: 16, core: 2. Of those that a mesh axis runs over, the one named last changes fastest.
Arguments:
- gate_input: bfloat16 [16384, 4096], P('ctx', 'ch'), may hold values from -6 to 6
- key_input: bfloat16 [16384, 4096], P('ctx', 'ch'), may hold values from -6 to 6
- value_input: bfloat16 [16384, 4096], P('ctx', 'ch'), may hold values from -6 to 6
- decay_rate: float32 [16, 4096], P(None, 'ch'), may hold values from 0.00012207031 to 0.26666667
- frequency: float32 [16, 4096], P(None, 'ch'), may hold values from 0 to 2.4
- residue: float32 [2, 16, 4096], P(None, None, 'ch'), may hold values from -2 to 2
- skip_gain: float32 [4096], P('ch'), may hold values from -3 to 3
- out_weight: bfloat16 [4096, 4096], P('ctx', 'ch'), may hold values from -0.09375 to 0.09375
Outputs:
- mixed: bfloat16 [16384, 4096], P('ctx', 'ch')
The draws below stay inside these ranges and needn't reach their ends.
All inputs are finite; a program needn't handle non-finite values.
Results may differ from the reference program's by a relative error of at most 0.014.
Values may be sent and summed in bfloat16 or wider, within the bound.
A program may use at most 128 MiB of HBM per device.

```python
import math
import jax
import jax.numpy as jnp
from jax import lax

D = 4096
MODES = 16
TOK_DEV = 256
SEQ = 16384


def draw_decay_rate(key, part):
    first, second, third = jax.random.split(jax.random.fold_in(key, 11), 3)
    slow_share = 0.5
    picked = jax.random.uniform(first, (MODES, D), jnp.float32) < slow_share
    slow = jnp.exp(jax.random.uniform(second, (MODES, D), jnp.float32, math.log(0.25 / SEQ), math.log(2.0 / SEQ)))
    fast = jnp.exp(jax.random.uniform(third, (MODES, D), jnp.float32, math.log(4.0 / SEQ), math.log(1.0 / 30.0)))
    return (8.0 * jnp.where(picked, slow, fast)).astype(jnp.float32)


def shard_levels(key, extent, cuts, smallest, high):
    def one(position, blocks):
        heights = jax.random.uniform(jax.random.fold_in(jax.random.fold_in(key, 6), position), (blocks,), jnp.float32, smallest / len(cuts), high / len(cuts))
        return jnp.repeat(jnp.exp(heights), extent[position] // blocks).reshape((-1,) + (1,) * (len(extent) - position - 1))

    loudness = one(*cuts[0])
    for cut in cuts[1:]:
        loudness = loudness * one(*cut)
    return loudness


def noise(own_key, extent, scale, bound, cuts=(), dtype=jnp.bfloat16):
    level = shard_levels(own_key, extent, cuts, -0.22, 0.18) if cuts else 1.0
    values = jax.random.normal(own_key, extent, jnp.float32) * scale * level
    return jnp.minimum(jnp.maximum(values, -bound), bound).astype(dtype)


def setup_inputs(seed: int = 0) -> dict:
    streams_of = jax.random.split(jax.random.key(seed), 9)
    gate_input = noise(streams_of[0], (SEQ, D), 1.0, 6.0, ((0, 64), (1, 8)))
    key_input = noise(streams_of[1], (SEQ, D), 1.0, 6.0, ((0, 64), (1, 8)))
    value_input = noise(streams_of[2], (SEQ, D), 1.0, 6.0, ((0, 64), (1, 8)))
    decay_rate = draw_decay_rate(jax.random.fold_in(streams_of[8], 71), 0)
    frequency = jnp.clip(2.4 * jax.random.uniform(streams_of[4], (MODES, D), jnp.float32) ** shard_levels(streams_of[4], (MODES, D), ((1, 8),), -0.2, 0.2), 0.0, 2.4)
    residue = noise(streams_of[5], (2, MODES, D), 0.35, 2.0, ((2, 8),), jnp.float32)
    skip_gain = noise(streams_of[6], (D,), 0.5, 3.0, ((0, 8),), jnp.float32)
    out_weight = noise(streams_of[7], (D, D), D ** -0.5, 0.09375, ((0, 64), (1, 8)))
    return {"gate_input": gate_input, "key_input": key_input, "value_input": value_input, "decay_rate": decay_rate, "frequency": frequency, "residue": residue, "skip_gain": skip_gain, "out_weight": out_weight}


def cmul(a_re, a_im, b_re, b_im):
    return (a_re * b_re - a_im * b_im, a_re * b_im + a_im * b_re)

def filter_tables(decay_rate, frequency, residue, block_len):
    damping = 0.125 * decay_rate
    turning = 0.125 * frequency
    scaling = jnp.sqrt(2.0 * damping)
    coef_re = scaling * residue[0]
    coef_im = scaling * residue[1]
    offsets = jnp.arange(block_len).astype(jnp.float32)

    def powers(counts):
        fading = jnp.exp(-damping[None] * counts[:, None, None])
        phase = turning[None] * counts[:, None, None]
        return (fading * jnp.cos(phase), fading * jnp.sin(phase))
    back_re, back_im = powers(block_len - 1.0 - offsets)
    ahead_re, ahead_im = powers(offsets + 1.0)
    out_re, out_im = cmul(coef_re[None], coef_im[None], ahead_re, ahead_im)
    lag_re, lag_im = powers(offsets)
    filt = lax.optimization_barrier(jnp.sum(coef_re[None] * lag_re - coef_im[None] * lag_im, axis=1))
    places = jnp.arange(block_len)
    differ = places[:, None] - places[None, :]
    picked = jnp.take(filt, jnp.maximum(differ, 0), axis=0)
    toeplitz = jnp.where((differ >= 0)[:, :, None], picked, jnp.zeros_like(picked))
    jump_re, jump_im = powers(jnp.full((1,), block_len).astype(jnp.float32))
    return (back_re, back_im, out_re, out_im, toeplitz, jump_re[0], jump_im[0])

def reference(gate_input, key_input, value_input, decay_rate, frequency, residue, skip_gain, out_weight):
    signal = key_input.astype(jnp.float32) * value_input.astype(jnp.float32)
    block_len = 16 if TOK_DEV % 16 == 0 else TOK_DEV
    back_re, back_im, out_re, out_im, toeplitz, jump_re, jump_im = filter_tables(decay_rate, frequency, residue, block_len)
    blocks = signal.reshape(SEQ // block_len, block_len, D)

    def advance(state, block):
        state_re, state_im = state
        far = lax.optimization_barrier(jnp.sum(out_re * state_re[None] - out_im * state_im[None], axis=1))
        near = jnp.einsum('tsc,sc->tc', toeplitz, block, precision=lax.Precision.HIGHEST)
        entry_re = lax.optimization_barrier(jnp.sum(back_re * block[:, None, :], axis=0))
        entry_im = lax.optimization_barrier(jnp.sum(back_im * block[:, None, :], axis=0))
        moved_re, moved_im = cmul(jump_re, jump_im, state_re, state_im)
        return ((moved_re + entry_re, moved_im + entry_im), far + near)
    zeros = jnp.zeros((MODES, D), jnp.float32)
    _, conv = lax.scan(advance, (zeros, zeros), blocks)
    conv = conv.reshape(SEQ, D)
    gated = (gate_input.astype(jnp.float32) * (conv + skip_gain[None, :] * signal)).astype(jnp.bfloat16)
    return jnp.dot(gated, out_weight, preferred_element_type=jnp.float32).astype(jnp.bfloat16)
```

```python
import functools

import jax
import jax.numpy as jnp
from jax import lax
from jax.experimental import pallas as pl
from jax.experimental.pallas import tpu as pltpu
from jax.sharding import PartitionSpec as P

MESH = pl.DeviceIdType.MESH
NX = 4
L = 16


def cmul(a_re, a_im, b_re, b_im):
    return (a_re * b_re - a_im * b_im, a_re * b_im + a_im * b_re)


def remote(src, dst, send_sem, recv_sem, device):
    return pltpu.make_async_remote_copy(
        src_ref=src,
        dst_ref=dst,
        send_sem=send_sem,
        recv_sem=recv_sem,
        device_id=device,
        device_id_type=MESH,
    )


def kernel(
    cfg,
    gate, key, value, decay, freq, residue, skip, weight,
    out,
    wfull, gall, sig, near, acc,
    pow_re, pow_im, out_re, out_im, toep, hpad,
    ent_re, ent_im, beg_re, beg_im, co_re, co_im,
    esend, esum, qpow, xin, zin, zin2, rsum, wsum, sx, sin,
    ax_s, ax_r, az_s, az_r, bz_s, bz_r, bx_s, bx_r, bh_s, bh_r,
    st_s, st_r, y_s, y_r,
):
    nz, ny, radix = cfg
    tok, chans = key.shape
    blocks = tok // L
    lanes = chans // NX
    rows = weight.shape[0]
    ra = rows // 2
    half = ra + (rows - ra) // 2
    zlim = ((1, nz // 2), (-1, nz // 2 - 1))

    ctx = lax.axis_index("ctx")
    ch = lax.axis_index("ch")
    z, x = ctx // NX, lax.rem(ctx, NX)
    y, core = ch // 2, lax.rem(ch, 2)

    def at_z(d):
        return (lax.rem(z + d + nz, nz) * NX + x, ch)

    def at_x(d):
        return (z * NX + lax.rem(x + d + NX, NX), ch)

    def at_y(d):
        return (ctx, lax.rem(y + d + ny, ny) * 2 + core)

    other = (ctx, y * 2 + 1 - core)

    near_z = list(range(1, radix))
    far_z = [1 + radix * m for m in range(radix)]
    z_peers = sorted({d % nz for d in [1, nz - 1] + near_z + far_z + [-d for d in near_z + far_z]})
    peers = [at_z(d) for d in z_peers] + [at_x(d) for d in range(1, NX)]
    if ny > 1:
        peers += [at_y(1), at_y(-1), other]
    barrier = pltpu.get_barrier_semaphore()
    for peer in peers:
        pl.semaphore_signal(barrier, inc=1, device_id=peer, device_id_type=MESH)

    wfull[ctx] = weight[...]
    damp = 0.125 * decay[...]
    turn = 0.125 * freq[...]
    fade = jnp.exp(-damp)
    lam_re, lam_im = fade * jnp.cos(turn), fade * jnp.sin(turn)
    scale = jnp.sqrt(2.0 * damp)
    co_re[...] = scale * residue[0]
    co_im[...] = scale * residue[1]
    cur = (jnp.ones_like(lam_re), jnp.zeros_like(lam_im))
    for k in range(L + 1):
        pow_re[k] = cur[0]
        pow_im[k] = cur[1]
        cur = cmul(cur[0], cur[1], lam_re, lam_im)

    pl.semaphore_wait(barrier, len(peers))

    def a_first(d):
        part = wfull.at[ctx, 0:ra]
        return remote(part, part, ax_s.at[d - 1], ax_r.at[d - 1], at_x(d))

    def a_step(dirn, k, sub, sgn, src_z):
        part = wfull.at[pl.ds(src_z * NX + 2 * sub, 2), 0:ra]
        return remote(part, part, az_s.at[dirn, k, sub], az_r.at[dirn, k, sub], at_z(sgn))

    def bz_step(dirn, k, sgn, src_z):
        part = wfull.at[src_z * NX + x, ra:rows]
        return remote(part, part, bz_s.at[dirn, k], bz_r.at[dirn, k], at_z(sgn))

    def bx_step(idx, src_z, side, from_x):
        part = wfull.at[src_z * NX + lax.rem(from_x + NX, NX), ra:rows]
        return remote(part, part, bx_s.at[idx, side], bx_r.at[idx, side], at_x(1 - 2 * side))

    def bh_step(idx, src_z, side, from_x):
        span = slice(ra, half) if side == 0 else slice(half, rows)
        part = wfull.at[src_z * NX + lax.rem(from_x + NX, NX), span]
        return remote(part, part, bh_s.at[idx, side], bh_r.at[idx, side], at_x(1 - 2 * side))

    def origin(sgn, k):
        return lax.rem(z - sgn * k + nz, nz)

    def halves(idx, src_z):
        for side in range(2):
            here = x - 1 if side == 0 else x + 1
            bx_step(idx, src_z, side, here).wait_recv()
            bh_step(idx, src_z, side, here).start()

    for d in (1, 3, 2):
        a_first(d).start()
    for dirn, (sgn, lim) in enumerate(zlim):
        bz_step(dirn, 1, sgn, z).start()
    for side in range(2):
        bx_step(0, z, side, x).start()

    jump_re, jump_im = pow_re[L], pow_im[L]
    esum[0] = jnp.zeros_like(jump_re)
    esum[1] = jnp.zeros_like(jump_re)

    def entries(b, _):
        at = pl.multiple_of(b * L, L)
        sig[pl.ds(at, L), :] = key[pl.ds(at, L), :].astype(jnp.float32) * value[
            pl.ds(at, L), :
        ].astype(jnp.float32)
        e_re = jnp.zeros(jump_re.shape, jnp.float32)
        e_im = jnp.zeros(jump_re.shape, jnp.float32)
        for s in range(L):
            row = sig[pl.ds(at + s, 1), :]
            e_re += pow_re[L - 1 - s] * row
            e_im += pow_im[L - 1 - s] * row
        ent_re[b] = e_re
        ent_im[b] = e_im
        m_re, m_im = cmul(pow_re[L], pow_im[L], esum[0], esum[1])
        esum[0] = m_re + e_re
        esum[1] = m_im + e_im
        return 0

    lax.fori_loop(0, blocks, entries, 0)
    for q in range(NX):
        for part in range(2):
            esend[q, part] = esum[part, :, q * lanes : (q + 1) * lanes]

    def x_out(d):
        to = lax.rem(x + d, NX)
        return remote(esend.at[to], xin.at[x], st_s.at[d - 1], st_r.at[d - 1], at_x(d))

    def z_out(i):
        d = near_z[i]
        return remote(rsum, zin.at[i], st_s.at[3 + i], st_r.at[3 + i], at_z(d))

    def z_out2(i):
        return remote(wsum, zin2.at[i], st_s.at[6 + i], st_r.at[6 + i], at_z(far_z[i]))

    def x_back(d):
        to = lax.rem(x + d, NX)
        return remote(sx.at[to], sin.at[x], st_s.at[9 + d], st_r.at[9 + d], at_x(d))

    for d in (1, 3, 2):
        x_out(d).start()
    xin[x] = esend[x]

    for d in (1, 3, 2):
        a_first(d).wait_recv()
    for dirn, (sgn, lim) in enumerate(zlim):
        for sub in range(2):
            a_step(dirn, 1, sub, sgn, z).start()

    fade_q = jnp.exp(-damp * float(tok))
    q_re = fade_q * jnp.cos(turn * float(tok))
    q_im = fade_q * jnp.sin(turn * float(tok))
    for q in range(NX):
        qpow[q, 0] = q_re[:, q * lanes : (q + 1) * lanes]
        qpow[q, 1] = q_im[:, q * lanes : (q + 1) * lanes]

    place = lax.broadcasted_iota(jnp.int32, (8, chans), 0)

    def out_tables(n, total):
        def row(ref, k):
            return jnp.broadcast_to(ref[k, pl.ds(n, 1), :], (8, chans))

        c_re = jnp.broadcast_to(co_re[pl.ds(n, 1), :], (8, chans))
        c_im = jnp.broadcast_to(co_im[pl.ds(n, 1), :], (8, chans))
        v = cmul(c_re, c_im, row(pow_re, 1), row(pow_im, 1))
        for bit in (1, 2, 4):
            w = cmul(*v, row(pow_re, bit), row(pow_im, bit))
            on = (place & bit) != 0
            v = (jnp.where(on, w[0], v[0]), jnp.where(on, w[1], v[1]))
        hi = cmul(*v, row(pow_re, 8), row(pow_im, 8))
        t_re = jnp.concatenate([v[0], hi[0]], axis=0)
        out_re[n] = t_re
        out_im[n] = jnp.concatenate([v[1], hi[1]], axis=0)
        return total + t_re

    def filters():
        later = lax.fori_loop(
            0, 16, out_tables, jnp.zeros((L, chans), jnp.float32)
        )
        hpad[0:L, :] = jnp.zeros((L, chans), jnp.float32)
        hpad[L - 1 : L, :] = jnp.sum(co_re[...], axis=0, keepdims=True) + skip[...]
        hpad[L : 2 * L, :] = later
        for s in range(L):
            toep[s] = hpad[L - 1 - s : 2 * L - 1 - s, :]

    def near_part(b, _):
        at = pl.multiple_of(b * L, L)
        total = jnp.zeros((L, chans), jnp.float32)
        for s in range(L):
            total += toep[s] * sig[pl.ds(at + s, 1), :]
        near[pl.ds(at, L), :] = total
        return 0

    def quarter_power(exp):
        one = (qpow[x, 0], qpow[x, 1])
        got = None
        while exp:
            if exp & 1:
                got = one if got is None else cmul(*got, *one)
            one = cmul(*one, *one)
            exp >>= 1
        return got

    def stage_row():
        for d in range(1, NX):
            x_out(d).wait_recv()
        one = (qpow[x, 0], qpow[x, 1])
        total = (xin[0, 0], xin[0, 1])
        for i in range(1, NX):
            moved = cmul(*total, *one)
            total = (moved[0] + xin[i, 0], moved[1] + xin[i, 1])
        rsum[0] = total[0]
        rsum[1] = total[1]
        for i in range(len(near_z)):
            z_out(i).start()

    def stage_near_z():
        total = (rsum[0], rsum[1])
        step = quarter_power(NX)
        power = None
        for i, d in enumerate(near_z):
            z_out(i).wait_recv()
            power = step if power is None else cmul(*power, *step)
            moved = cmul(*power, zin[i, 0], zin[i, 1])
            ok = z >= d
            total = (
                total[0] + jnp.where(ok, moved[0], 0.0),
                total[1] + jnp.where(ok, moved[1], 0.0),
            )
        wsum[0] = total[0]
        wsum[1] = total[1]
        for i in range(len(far_z)):
            z_out2(i).start()

    def stage_far_z():
        step = quarter_power(NX * radix)
        total, power = None, None
        for i, d in enumerate(far_z):
            z_out2(i).wait_recv()
            moved = (zin2[i, 0], zin2[i, 1])
            if i:
                power = step if power is None else cmul(*power, *step)
                moved = cmul(*power, *moved)
            ok = z >= d
            moved = (jnp.where(ok, moved[0], 0.0), jnp.where(ok, moved[1], 0.0))
            total = moved if total is None else (total[0] + moved[0], total[1] + moved[1])
        one = (qpow[x, 0], qpow[x, 1])
        for i in range(NX):
            sx[i, 0] = total[0]
            sx[i, 1] = total[1]
            moved = cmul(*total, *one)
            total = (moved[0] + xin[i, 0], moved[1] + xin[i, 1])
        for d in (1, 3, 2):
            x_back(d).start()
        sin[x] = sx[x]

    def stage_begin():
        for d in range(1, NX):
            x_back(d).wait_recv()
        for q in range(NX):
            beg_re[:, q * lanes : (q + 1) * lanes] = sin[q, 0]
            beg_im[:, q * lanes : (q + 1) * lanes] = sin[q, 1]

    def far_part(b, _):
        at = pl.multiple_of(b * L, L)
        total = near[pl.ds(at, L), :]
        for n in range(16):
            total += out_re[n] * beg_re[n : n + 1, :] - out_im[n] * beg_im[n : n + 1, :]
        gall[ch, pl.ds(at, L), :] = (gate[pl.ds(at, L), :].astype(jnp.float32) * total).astype(
            jnp.bfloat16
        )
        m_re, m_im = cmul(pow_re[L], pow_im[L], beg_re[...], beg_im[...])
        beg_re[...] = m_re + ent_re[b]
        beg_im[...] = m_im + ent_im[b]
        return 0

    chunk = tok // 2

    def y_copy(c, i):
        def block(dy, dev, lo=0, hi=chunk, mine=True):
            owner = lax.rem(y + dy + ny, ny) * 2 + core
            part = gall.at[owner, c * chunk + lo : c * chunk + hi]
            return remote(part, part, y_s.at[c, i], y_r.at[c, i], dev)

        mid = chunk // 2
        if i == 0:
            return block(0, other)
        if i == 1:
            return block(0, at_y(1))
        if i == 2:
            return block(0, at_y(-1))
        if i == 3:
            return block(-1, at_y(1), 0, mid)
        if i == 4:
            return block(1, at_y(-1), mid, chunk)
        if i == 5:
            return block(-1, other)
        if i == 6:
            return block(1, other)
        if i == 7:
            return block(2, other, 0, mid)
        return block(2, other, mid, chunk)

    def y_start(c):
        if ny > 1:
            for i in (1, 2, 0):
                y_copy(c, i).start()

    def y_forward(c):
        if ny > 1:
            for i in (1, 2):
                y_copy(c, i).wait_recv()
                y_copy(c, 2 + i).start()
                y_copy(c, 4 + i).start()

    def y_last(c):
        if ny > 1:
            for i in (3, 4):
                y_copy(c, i).wait_recv()
                y_copy(c, 4 + i).start()

    mid_block = blocks // 2

    def far_chunk(c):
        lax.fori_loop(c * mid_block, (c + 1) * mid_block, far_part, 0)
        y_start(c)

    def stage_1():
        stage_row()
        filters()

    def stage_2():
        stage_near_z()
        lax.fori_loop(0, mid_block, near_part, 0)

    def stage_3():
        stage_far_z()
        lax.fori_loop(mid_block, blocks, near_part, 0)

    def stage_4():
        stage_begin()
        far_chunk(0)

    def stage_5():
        far_chunk(1)

    def stage_6():
        y_forward(0)

    def stage_7():
        y_forward(1)
        y_last(0)

    def stage_8():
        y_last(1)

    stages = (stage_1, stage_2, stage_3, stage_4, stage_5, stage_6, stage_7, stage_8)

    def w_step(k):
        for dirn, (sgn, lim) in enumerate(zlim):

            @pl.when(k <= lim)
            def _():
                src_z = origin(sgn, k)
                idx = dirn * zlim[0][1] + k
                bz_step(dirn, k, sgn, src_z).wait_recv()

                @pl.when(k < lim)
                def _():
                    bz_step(dirn, k + 1, sgn, src_z).start()

                for side in range(2):
                    bx_step(idx, src_z, side, x).start()
                for sub in range(2):
                    a_step(dirn, k, sub, sgn, src_z).wait_recv()

                    @pl.when(k < lim)
                    def _():
                        a_step(dirn, k + 1, sub, sgn, src_z).start()

        before = k - 1
        halves(before, origin(1, before))

        @pl.when(jnp.logical_and(before >= 1, before <= zlim[1][1]))
        def _():
            halves(zlim[0][1] + before, origin(-1, before))

    steps = zlim[0][1]

    def tick(k, _):
        for i, stage in enumerate(stages):
            pl.when(k == i + 1)(stage)
        pl.when(k <= steps)(lambda: w_step(k))
        return 0

    lax.fori_loop(1, max(steps, len(stages)) + 1, tick, 0)
    halves(steps, origin(1, steps))

    for d in range(1, NX):
        a_first(d).wait_send()
        x_out(d).wait_send()
        x_back(d).wait_send()
    for i in range(len(near_z)):
        z_out(i).wait_send()
    for i in range(len(far_z)):
        z_out2(i).wait_send()

    def finish(k, _):
        for dirn, (sgn, lim) in enumerate(zlim):

            @pl.when(k <= lim)
            def _():
                src_z = origin(sgn, k - 1)
                bz_step(dirn, k, sgn, src_z).wait_send()
                for sub in range(2):
                    a_step(dirn, k, sub, sgn, src_z).wait_send()

        return 0

    lax.fori_loop(1, steps + 1, finish, 0)

    def finish_x(idx, _):
        off = jnp.where(idx <= steps, idx, steps - idx)
        src_z = lax.rem(z - off + nz, nz)
        for side in range(2):
            here = x - 1 if side == 0 else x + 1
            bx_step(idx, src_z, side, x).wait_send()
            bh_step(idx, src_z, side, here).wait_send()
            bh_step(idx, src_z, side, x + 2).wait_recv()
        return 0

    lax.fori_loop(0, nz, finish_x, 0)
    if ny > 1:
        for c in range(2):
            for i in (0, 5, 6, 7, 8):
                y_copy(c, i).wait_recv()
            for i in range(9):
                y_copy(c, i).wait_send()

    acc[...] = jnp.zeros_like(acc)
    per = chans // rows

    def project(j, _):
        w = wfull[pl.ds(j * per, per)].reshape(chans, chans)
        acc[...] += jnp.dot(gall[j], w, preferred_element_type=jnp.float32)
        return 0

    lax.fori_loop(0, gall.shape[0], project, 0)
    out[...] = acc[...].astype(out.dtype)


def on_device(
    gate_input, key_input, value_input, decay_rate, frequency, residue, skip_gain, out_weight
):
    n_ctx, n_ch = lax.axis_size("ctx"), lax.axis_size("ch")
    nz, ny = n_ctx // NX, n_ch // 2
    radix = {16: 4, 4: 2}[nz]
    tok, chans = key_input.shape
    rows = out_weight.shape[0]
    modes = decay_rate.shape[0]
    lanes = chans // NX
    f32, bf16 = jnp.float32, jnp.bfloat16
    dma = pltpu.SemaphoreType.DMA
    steps = nz // 2
    state = (2, modes, lanes)
    vmem = pl.BlockSpec(memory_space=pltpu.VMEM)
    scratch = [
        pltpu.VMEM((n_ctx, rows, chans), bf16),
        pltpu.VMEM((n_ch, tok, chans), bf16),
        pltpu.VMEM((tok, chans), f32),
        pltpu.VMEM((tok, chans), f32),
        pltpu.VMEM((tok, chans), f32),
        pltpu.VMEM((L + 1, modes, chans), f32),
        pltpu.VMEM((L + 1, modes, chans), f32),
        pltpu.VMEM((modes, L, chans), f32),
        pltpu.VMEM((modes, L, chans), f32),
        pltpu.VMEM((L, L, chans), f32),
        pltpu.VMEM((2 * L, chans), f32),
        pltpu.VMEM((tok // L, modes, chans), f32),
        pltpu.VMEM((tok // L, modes, chans), f32),
        pltpu.VMEM((modes, chans), f32),
        pltpu.VMEM((modes, chans), f32),
        pltpu.VMEM((modes, chans), f32),
        pltpu.VMEM((modes, chans), f32),
        pltpu.VMEM((NX,) + state, f32),
        pltpu.VMEM((2, modes, chans), f32),
        pltpu.VMEM((NX,) + state, f32),
        pltpu.VMEM((NX,) + state, f32),
        pltpu.VMEM((radix - 1,) + state, f32),
        pltpu.VMEM((radix,) + state, f32),
        pltpu.VMEM(state, f32),
        pltpu.VMEM(state, f32),
        pltpu.VMEM((NX,) + state, f32),
        pltpu.VMEM((NX,) + state, f32),
        dma((3,)),
        dma((3,)),
        dma((2, steps + 1, 2)),
        dma((2, steps + 1, 2)),
        dma((2, steps + 1)),
        dma((2, steps + 1)),
        dma((nz, 2)),
        dma((nz, 2)),
        dma((nz, 2)),
        dma((nz, 2)),
        dma((13,)),
        dma((13,)),
        dma((2, 9)),
        dma((2, 9)),
    ]
    return pl.pallas_call(
        functools.partial(kernel, (nz, ny, radix)),
        out_shape=jax.ShapeDtypeStruct((tok, chans), bf16),
        in_specs=[vmem] * 8,
        out_specs=vmem,
        scratch_shapes=scratch,
        compiler_params=pltpu.CompilerParams(
            collective_id=0, has_side_effects=True, vmem_limit_bytes=40 << 20
        ),
    )(
        gate_input,
        key_input,
        value_input,
        decay_rate,
        frequency,
        residue,
        skip_gain.reshape(1, chans),
        out_weight,
    )


def solution(mesh):
    placed = (
        P("ctx", "ch"),
        P("ctx", "ch"),
        P("ctx", "ch"),
        P(None, "ch"),
        P(None, "ch"),
        P(None, None, "ch"),
        P("ch"),
        P("ctx", "ch"),
    )
    return jax.shard_map(
        on_device, mesh=mesh, in_specs=placed, out_specs=P("ctx", "ch"), check_vma=False
    )
```

```python
import functools

import jax
import jax.numpy as jnp
from jax import lax
from jax.experimental import pallas as pl
from jax.experimental.pallas import tpu as pltpu
from jax.sharding import PartitionSpec as P

MESH = pl.DeviceIdType.MESH
NX = 4
L = 16
NB = 8
CHUNKS = 4


def cmul(a_re, a_im, b_re, b_im):
    return (a_re * b_re - a_im * b_im, a_re * b_im + a_im * b_re)


def remote(src, dst, send_sem, recv_sem, device):
    return pltpu.make_async_remote_copy(
        src_ref=src,
        dst_ref=dst,
        send_sem=send_sem,
        recv_sem=recv_sem,
        device_id=device,
        device_id_type=MESH,
    )


def small_trig(angle):
    q = angle * angle
    cos = 1.0 + q * (-1.0 / 2 + q * (1.0 / 24 + q * (-1.0 / 720 + q * (1.0 / 40320))))
    sin = angle * (1.0 + q * (-1.0 / 6 + q * (1.0 / 120 + q * (-1.0 / 5040 + q * (1.0 / 362880)))))
    return cos, sin


def kernel(
    cfg,
    gate_h, key_h, value_h, decay_h, freq_h, residue_h, skip_h, weight_h,
    out,
    wfull, gall, gate, key, value, decay, freq, residue, skip,
    sig, near, acc,
    pow_re, pow_im, out_re, out_im, toep, hpad,
    ent_re, ent_im, beg_re, beg_im, cur_re, cur_im, co_re, co_im,
    esend, qpow, xin, zin, rsum, sx, sin,
    in_s, know, ax_s, ax_r, az_s, az_r, bz_s, bz_r, bx_s, bx_r,
    xo_s, xo_r, zo_s, zo_r, xb_s, xb_r, y_s, y_r,
):
    nz, ny = cfg
    tok, chans = key.shape
    modes = decay.shape[0]
    blocks = tok // L
    nb = min(NB, blocks)
    lanes = chans // NX
    rows = wfull.shape[1]
    ra = rows // 2
    steps = nz // 2
    zlim = ((1, steps), (-1, steps - 1))
    chunks = min(CHUNKS, blocks)
    chunk = tok // chunks
    per_chunk = blocks // chunks

    ctx = lax.axis_index("ctx")
    ch = lax.axis_index("ch")
    z, x = ctx // NX, lax.rem(ctx, NX)
    y, core = ch // 2, lax.rem(ch, 2)

    def wrap(value, size):
        value = jnp.where(value < 0, value + size, value)
        return jnp.where(value >= size, value - size, value)

    z_at = {d: (wrap(z + d, nz) * NX + x, ch) for d in range(1 - nz, nz)}
    x_of = {d: wrap(x + d, NX) for d in range(1 - NX, NX)}
    x_at = {d: (z * NX + x_of[d], ch) for d in x_of}
    y_of = {d: wrap(y + d, ny) * 2 + core for d in (-1, 0, 1, 2)}
    y_at = {d: (ctx, y_of[d]) for d in y_of}
    at_z, at_x, at_y = z_at.get, x_at.get, y_at.get
    other = (ctx, y * 2 + 1 - core)

    fetches = [
        pltpu.make_async_copy(src, dst, in_s.at[i])
        for i, (src, dst) in enumerate(
            (
                (decay_h, decay),
                (freq_h, freq),
                (key_h, key),
                (value_h, value),
                (weight_h, wfull.at[ctx]),
                (residue_h, residue),
                (skip_h, skip),
                (gate_h, gate),
            )
        )
    ]
    for fetch in fetches:
        fetch.start()
    for d in range(nz - 1):
        zin[d] = jnp.zeros(zin.shape[1:], zin.dtype)

    peers = [at_z(1), at_z(-1)] + [at_x(d) for d in range(1, NX)]
    if ny > 1:
        peers += [at_y(1), at_y(-1), at_y(2), other]
    barrier = pltpu.get_barrier_semaphore()
    for peer in peers:
        pl.semaphore_signal(barrier, inc=1, device_id=peer, device_id_type=MESH)

    fetches[4].wait()
    pl.semaphore_wait(barrier, len(peers))

    def a_first(d):
        part = wfull.at[ctx, 0:ra]
        return remote(part, part, ax_s.at[d - 1], ax_r.at[d - 1], at_x(d))

    def bz_step(dirn, k, sgn, src_z):
        part = wfull.at[src_z * NX + x, ra:rows]
        return remote(part, part, bz_s.at[dirn, k], bz_r.at[dirn, k], at_z(sgn))

    def bx_step(idx, src_z, d, from_x):
        part = wfull.at[src_z * NX + from_x, ra:rows]
        return remote(part, part, bx_s.at[idx, d - 1], bx_r.at[idx, d - 1], at_x(d))

    def origin(sgn, k):
        return wrap(z - sgn * k, nz)

    for d in (2, 1, 3):
        a_first(d).start()
    for dirn, (sgn, lim) in enumerate(zlim):
        bz_step(dirn, 1, sgn, z).start()
    for d in (2, 1, 3):
        bx_step(0, z, d, x).start()

    def w_event(j):
        for dirn, (sgn, lim) in enumerate(zlim):

            @pl.when(j <= lim)
            def _():
                src_z = origin(sgn, j)
                bz_step(dirn, j, sgn, src_z).wait_recv()

                @pl.when(j < lim)
                def _():
                    bz_step(dirn, j + 1, sgn, src_z).start()

        @pl.when(j == 1)
        def _():
            for dirn, (sgn, lim) in enumerate(zlim):
                a_next(dirn, 1, 0, sgn, z).start()
            for d in range(1, NX):
                a_first(d).wait_recv()
                for dirn, (sgn, lim) in enumerate(zlim):
                    a_next(dirn, 1, d, sgn, z).start()

        k = j - 1
        for i in range(NX):
            for dirn, (sgn, lim) in enumerate(zlim):

                @pl.when(jnp.logical_and(k >= 1, k <= lim))
                def _():
                    src_z = origin(sgn, k)
                    a_next(dirn, k, i, sgn, src_z).wait_recv()

                    @pl.when(k < lim)
                    def _():
                        a_next(dirn, k + 1, i, sgn, src_z).start()

        for dirn, (sgn, lim) in enumerate(zlim):

            @pl.when(j <= lim)
            def _():
                for d in (2, 1, 3):
                    bx_step(dirn * steps + j, origin(sgn, j), d, x).start()

    def a_next(dirn, k, i, sgn, src_z):
        part = wfull.at[src_z * NX + x_of[-i], 0:ra]
        return remote(part, part, az_s.at[dirn, k, i], az_r.at[dirn, k, i], at_z(sgn))

    def tell(r):
        for d in (1 << r, -(1 << r)):
            pl.semaphore_signal(know.at[r], inc=1, device_id=at_z(d), device_id_type=MESH)

    rounds = steps.bit_length() - 1

    def hear(r):
        if r < rounds:
            pl.semaphore_wait(know.at[r], 2)
            if r + 1 < rounds:
                tell(r + 1)

    tell(0)

    fetches[0].wait()
    fetches[1].wait()
    damp = 0.125 * decay[...]
    turn = 0.125 * freq[...]
    fade = jnp.exp(-damp)
    cos, sine = small_trig(turn)
    lam_re, lam_im = fade * cos, fade * sine
    power = (jnp.ones_like(lam_re), jnp.zeros_like(lam_im))
    for k in range(L + 1):
        pow_re[k] = power[0]
        pow_im[k] = power[1]
        power = cmul(power[0], power[1], lam_re, lam_im)

    fetches[2].wait()
    fetches[3].wait()

    def signals(i, _):
        at = pl.multiple_of(i * L, L)
        both = key[pl.ds(at, L), :].astype(jnp.float32) * value[pl.ds(at, L), :].astype(jnp.float32)
        for g in range(NX):
            sig[g, pl.ds(at, L), :] = both[:, g * lanes : (g + 1) * lanes]
        return 0

    lax.fori_loop(0, blocks, signals, 0, unroll=2)

    def lane_group(g):
        return pl.ds(pl.multiple_of(g * lanes, lanes), lanes)

    groups = blocks // nb

    def entries(i, _):
        g = i // groups
        at, first = lane_group(g), pl.multiple_of(lax.rem(i, groups) * nb * L, nb * L)
        totals = [[jnp.zeros((modes, lanes), jnp.float32)] * 2 for _ in range(nb)]
        for s in range(L):
            p_re, p_im = pow_re[L - 1 - s, :, at], pow_im[L - 1 - s, :, at]
            for b in range(nb):
                row = sig[g, pl.ds(first + (b * L + s), 1), :]
                totals[b] = [totals[b][0] + p_re * row, totals[b][1] + p_im * row]
        for b in range(nb):
            ent_re[lax.rem(i, groups) * nb + b, :, at] = totals[b][0]
            ent_im[lax.rem(i, groups) * nb + b, :, at] = totals[b][1]
        return 0

    lax.fori_loop(0, NX * groups // 2, entries, 0)
    hear(0)
    lax.fori_loop(NX * groups // 2, NX * groups, entries, 0)

    def advance(b, state):
        moved = cmul(*state, pow_re[L], pow_im[L])
        return (moved[0] + ent_re[b], moved[1] + ent_im[b])

    empty = jnp.zeros((modes, chans), jnp.float32)
    whole = lax.fori_loop(0, blocks, advance, (empty, empty))
    for q in range(NX):
        for part in range(2):
            esend[q, part] = whole[part][:, q * lanes : (q + 1) * lanes]

    def x_out(d):
        to = x_of[d]
        return remote(esend.at[to], xin.at[x], xo_s.at[d - 1], xo_r.at[d - 1], at_x(d))

    def z_out(d):
        return remote(rsum, zin.at[d - 1], zo_s.at[d - 1], zo_r.at[d - 1], at_z(d))

    def x_back(d):
        to = x_of[d]
        return remote(sx.at[to], sin.at[x], xb_s.at[d - 1], xb_r.at[d - 1], at_x(d))

    for d in (2, 1, 3):
        x_out(d).start()
    xin[x] = esend[x]
    w_event(1)
    hear(1)

    fade_q = jnp.exp(-damp * float(tok))
    q_re = fade_q * jnp.cos(turn * float(tok))
    q_im = fade_q * jnp.sin(turn * float(tok))
    for q in range(NX):
        qpow[q, 0] = q_re[:, q * lanes : (q + 1) * lanes]
        qpow[q, 1] = q_im[:, q * lanes : (q + 1) * lanes]
    for i in (5, 6, 7):
        fetches[i].wait()
    scale = jnp.sqrt(2.0 * damp)
    co_re[...] = scale * residue[0]
    co_im[...] = scale * residue[1]

    place = lax.broadcasted_iota(jnp.int32, (8, chans), 0)

    def out_tables(n, total):
        def row(ref, k):
            return jnp.broadcast_to(ref[k, pl.ds(n, 1), :], (8, chans))

        c_re = jnp.broadcast_to(co_re[pl.ds(n, 1), :], (8, chans))
        c_im = jnp.broadcast_to(co_im[pl.ds(n, 1), :], (8, chans))
        v = cmul(c_re, c_im, row(pow_re, 1), row(pow_im, 1))
        for bit in (1, 2, 4):
            w = cmul(*v, row(pow_re, bit), row(pow_im, bit))
            on = (place & bit) != 0
            v = (jnp.where(on, w[0], v[0]), jnp.where(on, w[1], v[1]))
        hi = cmul(*v, row(pow_re, 8), row(pow_im, 8))
        t_re = jnp.concatenate([v[0], hi[0]], axis=0)
        out_re[n] = t_re
        out_im[n] = jnp.concatenate([v[1], hi[1]], axis=0)
        return total + t_re

    def filters():
        later = lax.fori_loop(0, modes, out_tables, jnp.zeros((L, chans), jnp.float32))
        hpad[0:L, :] = jnp.zeros((L, chans), jnp.float32)
        hpad[L - 1 : L, :] = jnp.sum(co_re[...], axis=0, keepdims=True) + skip[...]
        hpad[L : 2 * L, :] = later
        for s in range(L):
            toep[s] = hpad[L - 1 - s : 2 * L - 1 - s, :]

    def near_part(i, _):
        g = i // groups
        at, first = lane_group(g), pl.multiple_of(lax.rem(i, groups) * nb * L, nb * L)
        totals = [jnp.zeros((L, lanes), jnp.float32) for _ in range(nb)]
        for s in range(L):
            table = toep[s, :, at]
            for b in range(nb):
                totals[b] = totals[b] + table * sig[g, pl.ds(first + (b * L + s), 1), :]
        for b in range(nb):
            near[pl.ds(pl.multiple_of(first + b * L, L), L), at] = totals[b]
        return 0

    def stage_row():
        for d in range(1, NX):
            x_out(d).wait_recv()
        one = (qpow[x, 0], qpow[x, 1])
        total = (xin[0, 0], xin[0, 1])
        for i in range(1, NX):
            moved = cmul(*total, *one)
            total = (moved[0] + xin[i, 0], moved[1] + xin[i, 1])
        rsum[0] = total[0].astype(rsum.dtype)
        rsum[1] = total[1].astype(rsum.dtype)
        hear(2)
        for d in sorted(range(1, nz), key=lambda d: -min(d, nz - d)):
            pl.when(z + d < nz)(z_out(d).start)

    def stage_z():
        one = (qpow[x, 0], qpow[x, 1])
        two = cmul(*one, *one)
        step = cmul(*two, *two)
        for d in range(1, nz):
            pl.when(z >= d)(z_out(d).wait_recv)
        total = (jnp.zeros((modes, lanes), jnp.float32),) * 2
        for d in range(nz - 1, 0, -1):
            moved = cmul(*total, *step)
            total = (
                moved[0] + zin[d - 1, 0].astype(jnp.float32),
                moved[1] + zin[d - 1, 1].astype(jnp.float32),
            )
        for i in range(NX):
            sx[i, 0] = total[0]
            sx[i, 1] = total[1]
            moved = cmul(*total, *one)
            total = (moved[0] + xin[i, 0], moved[1] + xin[i, 1])
        for d in (2, 1, 3):
            x_back(d).start()
        sin[x] = sx[x]

    def stage_begin():
        for d in range(1, NX):
            x_back(d).wait_recv()
        for q in range(NX):
            cur_re[:, q * lanes : (q + 1) * lanes] = sin[q, 0]
            cur_im[:, q * lanes : (q + 1) * lanes] = sin[q, 1]

    def far_chunk(c):
        state = (cur_re[...], cur_im[...])
        for i in range(per_chunk):
            for g in range(NX):
                beg_re[g, i] = state[0][:, g * lanes : (g + 1) * lanes]
                beg_im[g, i] = state[1][:, g * lanes : (g + 1) * lanes]
            moved = cmul(*state, pow_re[L], pow_im[L])
            b = c * per_chunk + i
            state = (moved[0] + ent_re[b], moved[1] + ent_im[b])
        cur_re[...] = state[0]
        cur_im[...] = state[1]

        def far_part(g, _):
            at = lane_group(g)
            spots = [pl.ds(pl.multiple_of(c * chunk + i * L, L), L) for i in range(per_chunk)]
            totals = [near[spot, at] for spot in spots]
            for n in range(modes):
                t_re, t_im = out_re[n, :, at], out_im[n, :, at]
                for i in range(per_chunk):
                    totals[i] = totals[i] + (
                        t_re * beg_re[g, i, n : n + 1, :] - t_im * beg_im[g, i, n : n + 1, :]
                    )
            for spot, total in zip(spots, totals):
                gated = gate[spot, at].astype(jnp.float32) * total
                gall[ch, spot, at] = gated.astype(jnp.bfloat16)
            return 0

        lax.fori_loop(0, NX, far_part, 0)

    direct = chunks // 2

    def y_copy(c, i, straight):
        def block(dy, dev, lo=0, hi=chunk):
            at = c * chunk + lo
            part = gall.at[y_of[dy], pl.ds(pl.multiple_of(at, hi - lo), hi - lo)]
            return remote(part, part, y_s.at[c, i], y_r.at[c, i], dev)

        mid = chunk // 2
        if i == 0:
            return block(0, other)
        if i == 1:
            return block(0, at_y(1))
        if i == 2:
            return block(0, at_y(-1))
        if i == 3:
            return block(0, at_y(2)) if straight else block(-1, at_y(1), 0, mid)
        if i == 4:
            return block(1, at_y(-1), mid, chunk)
        if i == 5:
            return block(-1, other)
        if i == 6:
            return block(1, other)
        if i == 7:
            return block(2, other) if straight else block(2, other, 0, mid)
        return block(2, other, mid, chunk)

    def y_forward(c):
        if ny > 1:
            for i in (1, 2):
                y_copy(c, i, c >= direct).wait_recv()
                if c < direct:
                    y_copy(c, 2 + i, False).start()
                y_copy(c, 4 + i, c >= direct).start()

    def y_last(c):
        if ny > 1:
            if c < direct:
                for i in (3, 4):
                    y_copy(c, i, False).wait_recv()
                    y_copy(c, 4 + i, False).start()
            else:
                part = gall.at[y_of[2], c * chunk : (c + 1) * chunk]
                remote(part, part, y_s.at[c, 3], y_r.at[c, 3], at_y(2)).wait_recv()
                y_copy(c, 7, True).start()

    def far_all():
        def one(c, _):
            far_chunk(c)
            if ny > 1:
                for i in (1, 2, 0):
                    y_copy(c, i, False).start()

                @pl.when(c >= direct)
                def _():
                    y_copy(c, 3, True).start()

            return 0

        lax.fori_loop(0, chunks, one, 0)

    def stage_1():
        stage_row()
        filters()

    def stage_2():
        lax.fori_loop(0, NX * groups, near_part, 0)

    def stage_5():
        stage_begin()
        far_all()

    def stage_6():
        y_forward(0)
        y_forward(1)

    def stage_7():
        if chunks > 2:
            y_forward(2)
            y_forward(3)
        y_last(0)

    def stage_8():
        for c in range(1, chunks):
            y_last(c)

    stages = (stage_1, stage_2, stage_z, stage_5, stage_6, stage_7, stage_8)

    def tick(k, _):
        pl.when(k <= steps + 1)(lambda: w_event(k))
        for i, stage in enumerate(stages):
            pl.when(k == i + 2)(stage)
        return 0

    lax.fori_loop(2, max(steps, len(stages)) + 2, tick, 0)

    def across(idx, _):
        off = jnp.where(idx <= steps, idx, steps - idx)
        for d in range(1, NX):
            bx_step(idx, wrap(z - off, nz), d, x_of[-d]).wait_recv()
        return 0

    lax.fori_loop(0, nz, across, 0)

    per = chans // rows

    def project(dy, side, first=False):
        if ny > 1:
            j = y_of[dy] + (0 if side == 0 else 1 - 2 * core)
        else:
            j = 0
        w = wfull[pl.ds(j * per, per)].reshape(chans, chans)
        term = jnp.dot(gall[j], w, preferred_element_type=jnp.float32)
        acc[...] = term if first else acc[...] + term

    project(0, 0, True)
    if ny > 1:
        project(-1, 0)
        project(1, 0)
        for dy, side, waits in ((0, 1, (0,)), (-1, 1, (5,)), (1, 1, (6,)), (2, 0, ()), (2, 1, (7, 8))):
            for c in range(chunks):
                for i in waits:
                    if i < 8 or c < direct:
                        y_copy(c, i, c >= direct).wait_recv()
            project(dy, side)
    out[...] = acc[...].astype(out.dtype)

    for d in range(1, NX):
        a_first(d).wait_send()
        x_out(d).wait_send()
        x_back(d).wait_send()
    for d in range(1, nz):
        pl.when(z + d < nz)(z_out(d).wait_send)

    def finish(k, _):
        for dirn, (sgn, lim) in enumerate(zlim):

            @pl.when(k <= lim)
            def _():
                src_z = origin(sgn, k - 1)
                bz_step(dirn, k, sgn, src_z).wait_send()
                for i in range(NX):
                    a_next(dirn, k, i, sgn, src_z).wait_send()

        return 0

    lax.fori_loop(1, steps + 1, finish, 0)

    def finish_x(idx, _):
        off = jnp.where(idx <= steps, idx, steps - idx)
        for d in range(1, NX):
            bx_step(idx, wrap(z - off, nz), d, x).wait_send()
        return 0

    lax.fori_loop(0, nz, finish_x, 0)
    if ny > 1:
        for c in range(chunks):
            for i in range(9):
                if c < direct or i not in (4, 8):
                    y_copy(c, i, c >= direct).wait_send()


def on_device(
    gate_input, key_input, value_input, decay_rate, frequency, residue, skip_gain, out_weight
):
    n_ctx, n_ch = lax.axis_size("ctx"), lax.axis_size("ch")
    nz, ny = n_ctx // NX, n_ch // 2
    tok, chans = key_input.shape
    rows = out_weight.shape[0]
    modes = decay_rate.shape[0]
    lanes = chans // NX
    blocks = tok // L
    chunks = min(CHUNKS, blocks)
    f32, bf16 = jnp.float32, jnp.bfloat16
    dma = pltpu.SemaphoreType.DMA
    steps = nz // 2
    state = (2, modes, lanes)
    table = pltpu.VMEM((L + 1, modes, chans), f32)
    panel = pltpu.VMEM((tok, chans), f32)
    single = pltpu.VMEM((modes, chans), f32)
    scratch = [
        pltpu.VMEM((n_ctx, rows, chans), bf16),
        pltpu.VMEM((n_ch, tok, chans), bf16),
        pltpu.VMEM((tok, chans), bf16),
        pltpu.VMEM((tok, chans), bf16),
        pltpu.VMEM((tok, chans), bf16),
        single,
        single,
        pltpu.VMEM((2, modes, chans), f32),
        pltpu.VMEM((1, chans), f32),
        pltpu.VMEM((NX, tok, lanes), f32),
        panel,
        panel,
        table,
        table,
        pltpu.VMEM((modes, L, chans), f32),
        pltpu.VMEM((modes, L, chans), f32),
        pltpu.VMEM((L, L, chans), f32),
        pltpu.VMEM((2 * L, chans), f32),
        pltpu.VMEM((blocks, modes, chans), f32),
        pltpu.VMEM((blocks, modes, chans), f32),
        pltpu.VMEM((NX, blocks // chunks, modes, lanes), f32),
        pltpu.VMEM((NX, blocks // chunks, modes, lanes), f32),
        single,
        single,
        single,
        single,
        pltpu.VMEM((NX,) + state, f32),
        pltpu.VMEM((NX,) + state, f32),
        pltpu.VMEM((NX,) + state, f32),
        pltpu.VMEM((nz - 1,) + state, bf16),
        pltpu.VMEM(state, bf16),
        pltpu.VMEM((NX,) + state, f32),
        pltpu.VMEM((NX,) + state, f32),
        dma((8,)),
        pltpu.SemaphoreType.REGULAR((4,)),
        dma((3,)),
        dma((3,)),
        dma((2, steps + 1, NX)),
        dma((2, steps + 1, NX)),
        dma((2, steps + 1)),
        dma((2, steps + 1)),
        dma((nz, 3)),
        dma((nz, 3)),
        dma((3,)),
        dma((3,)),
        dma((nz - 1,)),
        dma((nz - 1,)),
        dma((3,)),
        dma((3,)),
        dma((chunks, 9)),
        dma((chunks, 9)),
    ]
    return pl.pallas_call(
        functools.partial(kernel, (nz, ny)),
        out_shape=jax.ShapeDtypeStruct((tok, chans), bf16),
        in_specs=[pl.BlockSpec(memory_space=pltpu.HBM)] * 8,
        out_specs=pl.BlockSpec(memory_space=pltpu.VMEM),
        scratch_shapes=scratch,
        compiler_params=pltpu.CompilerParams(
            collective_id=0, has_side_effects=True, vmem_limit_bytes=40 << 20
        ),
    )(
        *(
            pltpu.with_memory_space_constraint(array, pltpu.HBM)
            for array in (
                gate_input,
                key_input,
                value_input,
                decay_rate,
                frequency,
                residue,
                skip_gain.reshape(1, chans),
                out_weight,
            )
        )
    )


def solution(mesh):
    placed = (
        P("ctx", "ch"),
        P("ctx", "ch"),
        P("ctx", "ch"),
        P(None, "ch"),
        P(None, "ch"),
        P(None, None, "ch"),
        P("ch"),
        P("ctx", "ch"),
    )
    return jax.shard_map(
        on_device, mesh=mesh, in_specs=placed, out_specs=P("ctx", "ch"), check_vma=False
    )
```

```python
import functools

import jax
import jax.numpy as jnp
from jax import lax
from jax.experimental import pallas as pl
from jax.experimental.pallas import tpu as pltpu
from jax.sharding import PartitionSpec as P

MESH = pl.DeviceIdType.MESH
NX = 4
L = 16
NB = 8
CHUNKS = 4


def cmul(a_re, a_im, b_re, b_im):
    return (a_re * b_re - a_im * b_im, a_re * b_im + a_im * b_re)


def remote(src, dst, send_sem, recv_sem, device):
    return pltpu.make_async_remote_copy(
        src_ref=src,
        dst_ref=dst,
        send_sem=send_sem,
        recv_sem=recv_sem,
        device_id=device,
        device_id_type=MESH,
    )


def small_trig(angle):
    q = angle * angle
    cos = 1.0 + q * (-1.0 / 2 + q * (1.0 / 24 + q * (-1.0 / 720 + q * (1.0 / 40320))))
    sin = angle * (1.0 + q * (-1.0 / 6 + q * (1.0 / 120 + q * (-1.0 / 5040 + q * (1.0 / 362880)))))
    return cos, sin


def kernel(
    cfg,
    gate_h, key_h, value_h, decay_h, freq_h, residue_h, skip_h, weight_h,
    out,
    wfull, gall, gate, key, value, decay, freq, residue, skip,
    sig, near, acc,
    pow_re, pow_im, out_re, out_im, toep, hpad,
    ent_re, ent_im, beg_re, beg_im, cur_re, cur_im, co_re, co_im,
    esend, qpow, xin, zin, rsum, sx, sin,
    in_s, know, ax_s, ax_r, az_s, az_r, bz_s, bz_r, bx_s, bx_r,
    xo_s, xo_r, zo_s, zo_r, xb_s, xb_r, y_s, y_r,
):
    nz, ny = cfg
    tok, chans = key.shape
    modes = decay.shape[0]
    blocks = tok // L
    nb = min(NB, blocks)
    lanes = chans // NX
    rows = wfull.shape[1]
    ra = rows // 4
    steps = nz // 2
    zlim = ((1, steps), (-1, steps - 1))
    chunks = min(CHUNKS, blocks)
    chunk = tok // chunks
    per_chunk = blocks // chunks

    ctx = lax.axis_index("ctx")
    ch = lax.axis_index("ch")
    z, x = ctx // NX, lax.rem(ctx, NX)
    y, core = ch // 2, lax.rem(ch, 2)

    def wrap(value, size):
        value = jnp.where(value < 0, value + size, value)
        return jnp.where(value >= size, value - size, value)

    z_at = {d: (wrap(z + d, nz) * NX + x, ch) for d in range(1 - nz, nz)}
    x_of = {d: wrap(x + d, NX) for d in range(1 - NX, NX)}
    x_at = {d: (z * NX + x_of[d], ch) for d in x_of}
    y_of = {d: wrap(y + d, ny) * 2 + core for d in (-1, 0, 1, 2)}
    y_at = {d: (ctx, y_of[d]) for d in y_of}
    at_z, at_x, at_y = z_at.get, x_at.get, y_at.get
    other = (ctx, y * 2 + 1 - core)

    fetches = [
        pltpu.make_async_copy(src, dst, in_s.at[i])
        for i, (src, dst) in enumerate(
            (
                (decay_h, decay),
                (freq_h, freq),
                (key_h, key),
                (value_h, value),
                (weight_h, wfull.at[ctx]),
                (residue_h, residue),
                (skip_h, skip),
                (gate_h, gate),
            )
        )
    ]
    for fetch in fetches:
        fetch.start()
    for d in range(nz - 1):
        zin[d] = jnp.zeros(zin.shape[1:], zin.dtype)

    peers = [at_z(1), at_z(-1)] + [at_x(d) for d in range(1, NX)]
    if ny > 1:
        peers += [at_y(1), at_y(-1), at_y(2), other]
    barrier = pltpu.get_barrier_semaphore()
    for peer in peers:
        pl.semaphore_signal(barrier, inc=1, device_id=peer, device_id_type=MESH)

    fetches[4].wait()
    pl.semaphore_wait(barrier, len(peers))

    def a_first(d):
        part = wfull.at[ctx, 0:ra]
        return remote(part, part, ax_s.at[d - 1], ax_r.at[d - 1], at_x(d))

    def bz_step(dirn, k, sgn, src_z):
        part = wfull.at[src_z * NX + x, ra:rows]
        return remote(part, part, bz_s.at[dirn, k], bz_r.at[dirn, k], at_z(sgn))

    def bx_step(idx, src_z, d, from_x):
        part = wfull.at[src_z * NX + from_x, ra:rows]
        return remote(part, part, bx_s.at[idx, d - 1], bx_r.at[idx, d - 1], at_x(d))

    def origin(sgn, k):
        return wrap(z - sgn * k, nz)

    for d in (2, 1, 3):
        a_first(d).start()
    for dirn, (sgn, lim) in enumerate(zlim):
        bz_step(dirn, 1, sgn, z).start()
    for d in (2, 1, 3):
        bx_step(0, z, d, x).start()

    def w_event(j):
        for dirn, (sgn, lim) in enumerate(zlim):

            @pl.when(j <= lim)
            def _():
                src_z = origin(sgn, j)
                bz_step(dirn, j, sgn, src_z).wait_recv()

                @pl.when(j < lim)
                def _():
                    bz_step(dirn, j + 1, sgn, src_z).start()

                for d in (2, 1, 3):
                    bx_step(dirn * steps + j, src_z, d, x).start()

        @pl.when(j == 1)
        def _():
            for dirn, (sgn, lim) in enumerate(zlim):
                a_next(dirn, 1, 0, sgn, z).start()
            for d in range(1, NX):
                a_first(d).wait_recv()
                for dirn, (sgn, lim) in enumerate(zlim):
                    a_next(dirn, 1, d, sgn, z).start()

        k = j - 1
        for i in range(NX):
            for dirn, (sgn, lim) in enumerate(zlim):

                @pl.when(jnp.logical_and(k >= 1, k <= lim))
                def _():
                    src_z = origin(sgn, k)
                    a_next(dirn, k, i, sgn, src_z).wait_recv()

                    @pl.when(k < lim)
                    def _():
                        a_next(dirn, k + 1, i, sgn, src_z).start()

    def a_next(dirn, k, i, sgn, src_z):
        part = wfull.at[src_z * NX + x_of[-i], 0:ra]
        return remote(part, part, az_s.at[dirn, k, i], az_r.at[dirn, k, i], at_z(sgn))

    def tell(r):
        for d in (1 << r, -(1 << r)):
            pl.semaphore_signal(know.at[r], inc=1, device_id=at_z(d), device_id_type=MESH)

    rounds = steps.bit_length() - 1

    def hear(r):
        if r < rounds:
            pl.semaphore_wait(know.at[r], 2)
            if r + 1 < rounds:
                tell(r + 1)

    tell(0)

    fetches[0].wait()
    fetches[1].wait()
    damp = 0.125 * decay[...]
    turn = 0.125 * freq[...]
    fade = jnp.exp(-damp)
    cos, sine = small_trig(turn)
    lam_re, lam_im = fade * cos, fade * sine
    power = (jnp.ones_like(lam_re), jnp.zeros_like(lam_im))
    for k in range(L + 1):
        pow_re[k] = power[0]
        pow_im[k] = power[1]
        power = cmul(power[0], power[1], lam_re, lam_im)

    fetches[2].wait()
    fetches[3].wait()

    def signals(i, _):
        at = pl.multiple_of(i * L, L)
        both = key[pl.ds(at, L), :].astype(jnp.float32) * value[pl.ds(at, L), :].astype(jnp.float32)
        for g in range(NX):
            sig[g, pl.ds(at, L), :] = both[:, g * lanes : (g + 1) * lanes]
        return 0

    lax.fori_loop(0, blocks, signals, 0, unroll=2)

    def lane_group(g):
        return pl.ds(pl.multiple_of(g * lanes, lanes), lanes)

    groups = blocks // nb

    def entries(i, _):
        g = i // groups
        at, first = lane_group(g), pl.multiple_of(lax.rem(i, groups) * nb * L, nb * L)
        totals = [[jnp.zeros((modes, lanes), jnp.float32)] * 2 for _ in range(nb)]
        for s in range(L):
            p_re, p_im = pow_re[L - 1 - s, :, at], pow_im[L - 1 - s, :, at]
            for b in range(nb):
                row = sig[g, pl.ds(first + (b * L + s), 1), :]
                totals[b] = [totals[b][0] + p_re * row, totals[b][1] + p_im * row]
        for b in range(nb):
            ent_re[lax.rem(i, groups) * nb + b, :, at] = totals[b][0]
            ent_im[lax.rem(i, groups) * nb + b, :, at] = totals[b][1]
        return 0

    lax.fori_loop(0, NX * groups // 2, entries, 0)
    hear(0)
    w_event(1)
    lax.fori_loop(NX * groups // 2, NX * groups, entries, 0)

    def advance(b, state):
        moved = cmul(*state, pow_re[L], pow_im[L])
        return (moved[0] + ent_re[b], moved[1] + ent_im[b])

    empty = jnp.zeros((modes, chans), jnp.float32)
    whole = lax.fori_loop(0, blocks, advance, (empty, empty))
    for q in range(NX):
        for part in range(2):
            esend[q, part] = whole[part][:, q * lanes : (q + 1) * lanes]

    def x_out(d):
        to = x_of[d]
        return remote(esend.at[to], xin.at[x], xo_s.at[d - 1], xo_r.at[d - 1], at_x(d))

    def z_out(d):
        return remote(rsum, zin.at[d - 1], zo_s.at[d - 1], zo_r.at[d - 1], at_z(d))

    def x_back(d):
        to = x_of[d]
        return remote(sx.at[to], sin.at[x], xb_s.at[d - 1], xb_r.at[d - 1], at_x(d))

    for d in (2, 1, 3):
        x_out(d).start()
    xin[x] = esend[x]
    hear(1)

    fade_q = jnp.exp(-damp * float(tok))
    q_re = fade_q * jnp.cos(turn * float(tok))
    q_im = fade_q * jnp.sin(turn * float(tok))
    for q in range(NX):
        qpow[q, 0] = q_re[:, q * lanes : (q + 1) * lanes]
        qpow[q, 1] = q_im[:, q * lanes : (q + 1) * lanes]
    for i in (5, 6, 7):
        fetches[i].wait()
    scale = jnp.sqrt(2.0 * damp)
    co_re[...] = scale * residue[0]
    co_im[...] = scale * residue[1]

    place = lax.broadcasted_iota(jnp.int32, (8, chans), 0)

    def out_tables(n, total):
        def row(ref, k):
            return jnp.broadcast_to(ref[k, pl.ds(n, 1), :], (8, chans))

        c_re = jnp.broadcast_to(co_re[pl.ds(n, 1), :], (8, chans))
        c_im = jnp.broadcast_to(co_im[pl.ds(n, 1), :], (8, chans))
        v = cmul(c_re, c_im, row(pow_re, 1), row(pow_im, 1))
        for bit in (1, 2, 4):
            w = cmul(*v, row(pow_re, bit), row(pow_im, bit))
            on = (place & bit) != 0
            v = (jnp.where(on, w[0], v[0]), jnp.where(on, w[1], v[1]))
        hi = cmul(*v, row(pow_re, 8), row(pow_im, 8))
        t_re = jnp.concatenate([v[0], hi[0]], axis=0)
        out_re[n] = t_re
        out_im[n] = jnp.concatenate([v[1], hi[1]], axis=0)
        return total + t_re

    def filters():
        later = lax.fori_loop(0, modes, out_tables, jnp.zeros((L, chans), jnp.float32))
        hpad[0:L, :] = jnp.zeros((L, chans), jnp.float32)
        hpad[L - 1 : L, :] = jnp.sum(co_re[...], axis=0, keepdims=True) + skip[...]
        hpad[L : 2 * L, :] = later
        for s in range(L):
            toep[s] = hpad[L - 1 - s : 2 * L - 1 - s, :]

    def near_part(i, _):
        g = i // groups
        at, first = lane_group(g), pl.multiple_of(lax.rem(i, groups) * nb * L, nb * L)
        totals = [jnp.zeros((L, lanes), jnp.float32) for _ in range(nb)]
        for s in range(L):
            table = toep[s, :, at]
            for b in range(nb):
                totals[b] = totals[b] + table * sig[g, pl.ds(first + (b * L + s), 1), :]
        for b in range(nb):
            near[pl.ds(pl.multiple_of(first + b * L, L), L), at] = totals[b]
        return 0

    def stage_row():
        for d in range(1, NX):
            x_out(d).wait_recv()
        one = (qpow[x, 0], qpow[x, 1])
        total = (xin[0, 0], xin[0, 1])
        for i in range(1, NX):
            moved = cmul(*total, *one)
            total = (moved[0] + xin[i, 0], moved[1] + xin[i, 1])
        rsum[0] = total[0].astype(rsum.dtype)
        rsum[1] = total[1].astype(rsum.dtype)
        hear(2)
        for d in sorted(range(1, nz), key=lambda d: -min(d, nz - d)):
            pl.when(z + d < nz)(z_out(d).start)

    def stage_z():
        one = (qpow[x, 0], qpow[x, 1])
        two = cmul(*one, *one)
        step = cmul(*two, *two)
        for d in range(1, nz):
            pl.when(z >= d)(z_out(d).wait_recv)
        total = (jnp.zeros((modes, lanes), jnp.float32),) * 2
        for d in range(nz - 1, 0, -1):
            moved = cmul(*total, *step)
            total = (
                moved[0] + zin[d - 1, 0].astype(jnp.float32),
                moved[1] + zin[d - 1, 1].astype(jnp.float32),
            )
        for i in range(NX):
            sx[i, 0] = total[0]
            sx[i, 1] = total[1]
            moved = cmul(*total, *one)
            total = (moved[0] + xin[i, 0], moved[1] + xin[i, 1])
        for d in (2, 1, 3):
            x_back(d).start()
        sin[x] = sx[x]

    def stage_begin():
        for d in range(1, NX):
            x_back(d).wait_recv()
        for q in range(NX):
            cur_re[:, q * lanes : (q + 1) * lanes] = sin[q, 0]
            cur_im[:, q * lanes : (q + 1) * lanes] = sin[q, 1]

    def far_chunk(c):
        state = (cur_re[...], cur_im[...])
        for i in range(per_chunk):
            for g in range(NX):
                beg_re[g, i] = state[0][:, g * lanes : (g + 1) * lanes]
                beg_im[g, i] = state[1][:, g * lanes : (g + 1) * lanes]
            moved = cmul(*state, pow_re[L], pow_im[L])
            b = c * per_chunk + i
            state = (moved[0] + ent_re[b], moved[1] + ent_im[b])
        cur_re[...] = state[0]
        cur_im[...] = state[1]

        def far_part(g, _):
            at = lane_group(g)
            spots = [pl.ds(pl.multiple_of(c * chunk + i * L, L), L) for i in range(per_chunk)]
            totals = [near[spot, at] for spot in spots]
            for n in range(modes):
                t_re, t_im = out_re[n, :, at], out_im[n, :, at]
                for i in range(per_chunk):
                    totals[i] = totals[i] + (
                        t_re * beg_re[g, i, n : n + 1, :] - t_im * beg_im[g, i, n : n + 1, :]
                    )
            for spot, total in zip(spots, totals):
                gated = gate[spot, at].astype(jnp.float32) * total
                gall[ch, spot, at] = gated.astype(jnp.bfloat16)
            return 0

        lax.fori_loop(0, NX, far_part, 0)

    direct = chunks // 2

    def y_copy(c, i, straight):
        def block(dy, dev, lo=0, hi=chunk):
            at = c * chunk + lo
            part = gall.at[y_of[dy], pl.ds(pl.multiple_of(at, hi - lo), hi - lo)]
            return remote(part, part, y_s.at[c, i], y_r.at[c, i], dev)

        mid = chunk // 2
        if i == 0:
            return block(0, other)
        if i == 1:
            return block(0, at_y(1))
        if i == 2:
            return block(0, at_y(-1))
        if i == 3:
            return block(0, at_y(2)) if straight else block(-1, at_y(1), 0, mid)
        if i == 4:
            return block(1, at_y(-1), mid, chunk)
        if i == 5:
            return block(-1, other)
        if i == 6:
            return block(1, other)
        if i == 7:
            return block(2, other) if straight else block(2, other, 0, mid)
        return block(2, other, mid, chunk)

    def y_forward(c):
        if ny > 1:
            for i in (1, 2):
                y_copy(c, i, c >= direct).wait_recv()
                if c < direct:
                    y_copy(c, 2 + i, False).start()
                y_copy(c, 4 + i, c >= direct).start()

    def y_last(c):
        if ny > 1:
            if c < direct:
                for i in (3, 4):
                    y_copy(c, i, False).wait_recv()
                    y_copy(c, 4 + i, False).start()
            else:
                part = gall.at[y_of[2], c * chunk : (c + 1) * chunk]
                remote(part, part, y_s.at[c, 3], y_r.at[c, 3], at_y(2)).wait_recv()
                y_copy(c, 7, True).start()

    def far_all():
        def one(c, _):
            far_chunk(c)
            if ny > 1:
                for i in (1, 2, 0):
                    y_copy(c, i, False).start()

                @pl.when(c >= direct)
                def _():
                    y_copy(c, 3, True).start()

            return 0

        lax.fori_loop(0, chunks, one, 0)

    def stage_1():
        stage_row()
        filters()

    def stage_2():
        lax.fori_loop(0, NX * groups, near_part, 0)

    def stage_5():
        stage_begin()
        far_all()

    def stage_6():
        y_forward(0)
        y_forward(1)

    def stage_7():
        if chunks > 2:
            y_forward(2)
            y_forward(3)
        y_last(0)

    def stage_8():
        for c in range(1, chunks):
            y_last(c)

    stages = (stage_1, stage_2, stage_z, stage_5, stage_6, stage_7, stage_8)

    def tick(k, _):
        pl.when(k <= steps + 1)(lambda: w_event(k))
        for i, stage in enumerate(stages):
            pl.when(k == i + 2)(stage)
        return 0

    lax.fori_loop(2, max(steps, len(stages)) + 2, tick, 0)

    def across(idx, _):
        off = jnp.where(idx <= steps, idx, steps - idx)
        for d in range(1, NX):
            bx_step(idx, wrap(z - off, nz), d, x_of[-d]).wait_recv()
        return 0

    lax.fori_loop(0, nz, across, 0)

    per = chans // rows

    def project(dy, side, first=False):
        if ny > 1:
            j = y_of[dy] + (0 if side == 0 else 1 - 2 * core)
        else:
            j = 0
        w = wfull[pl.ds(j * per, per)].reshape(chans, chans)
        term = jnp.dot(gall[j], w, preferred_element_type=jnp.float32)
        acc[...] = term if first else acc[...] + term

    project(0, 0, True)
    if ny > 1:
        project(-1, 0)
        project(1, 0)
        for dy, side, waits in ((0, 1, (0,)), (-1, 1, (5,)), (1, 1, (6,)), (2, 0, ()), (2, 1, (7, 8))):
            for c in range(chunks):
                for i in waits:
                    if i < 8 or c < direct:
                        y_copy(c, i, c >= direct).wait_recv()
            project(dy, side)
    out[...] = acc[...].astype(out.dtype)

    for d in range(1, NX):
        a_first(d).wait_send()
        x_out(d).wait_send()
        x_back(d).wait_send()
    for d in range(1, nz):
        pl.when(z + d < nz)(z_out(d).wait_send)

    def finish(k, _):
        for dirn, (sgn, lim) in enumerate(zlim):

            @pl.when(k <= lim)
            def _():
                src_z = origin(sgn, k - 1)
                bz_step(dirn, k, sgn, src_z).wait_send()
                for i in range(NX):
                    a_next(dirn, k, i, sgn, src_z).wait_send()

        return 0

    lax.fori_loop(1, steps + 1, finish, 0)

    def finish_x(idx, _):
        off = jnp.where(idx <= steps, idx, steps - idx)
        for d in range(1, NX):
            bx_step(idx, wrap(z - off, nz), d, x).wait_send()
        return 0

    lax.fori_loop(0, nz, finish_x, 0)
    if ny > 1:
        for c in range(chunks):
            for i in range(9):
                if c < direct or i not in (4, 8):
                    y_copy(c, i, c >= direct).wait_send()


def on_device(
    gate_input, key_input, value_input, decay_rate, frequency, residue, skip_gain, out_weight
):
    n_ctx, n_ch = lax.axis_size("ctx"), lax.axis_size("ch")
    nz, ny = n_ctx // NX, n_ch // 2
    tok, chans = key_input.shape
    rows = out_weight.shape[0]
    modes = decay_rate.shape[0]
    lanes = chans // NX
    blocks = tok // L
    chunks = min(CHUNKS, blocks)
    f32, bf16 = jnp.float32, jnp.bfloat16
    dma = pltpu.SemaphoreType.DMA
    steps = nz // 2
    state = (2, modes, lanes)
    table = pltpu.VMEM((L + 1, modes, chans), f32)
    panel = pltpu.VMEM((tok, chans), f32)
    single = pltpu.VMEM((modes, chans), f32)
    scratch = [
        pltpu.VMEM((n_ctx, rows, chans), bf16),
        pltpu.VMEM((n_ch, tok, chans), bf16),
        pltpu.VMEM((tok, chans), bf16),
        pltpu.VMEM((tok, chans), bf16),
        pltpu.VMEM((tok, chans), bf16),
        single,
        single,
        pltpu.VMEM((2, modes, chans), f32),
        pltpu.VMEM((1, chans), f32),
        pltpu.VMEM((NX, tok, lanes), f32),
        panel,
        panel,
        table,
        table,
        pltpu.VMEM((modes, L, chans), f32),
        pltpu.VMEM((modes, L, chans), f32),
        pltpu.VMEM((L, L, chans), f32),
        pltpu.VMEM((2 * L, chans), f32),
        pltpu.VMEM((blocks, modes, chans), f32),
        pltpu.VMEM((blocks, modes, chans), f32),
        pltpu.VMEM((NX, blocks // chunks, modes, lanes), f32),
        pltpu.VMEM((NX, blocks // chunks, modes, lanes), f32),
        single,
        single,
        single,
        single,
        pltpu.VMEM((NX,) + state, f32),
        pltpu.VMEM((NX,) + state, f32),
        pltpu.VMEM((NX,) + state, f32),
        pltpu.VMEM((nz - 1,) + state, bf16),
        pltpu.VMEM(state, bf16),
        pltpu.VMEM((NX,) + state, f32),
        pltpu.VMEM((NX,) + state, f32),
        dma((8,)),
        pltpu.SemaphoreType.REGULAR((4,)),
        dma((3,)),
        dma((3,)),
        dma((2, steps + 1, NX)),
        dma((2, steps + 1, NX)),
        dma((2, steps + 1)),
        dma((2, steps + 1)),
        dma((nz, 3)),
        dma((nz, 3)),
        dma((3,)),
        dma((3,)),
        dma((nz - 1,)),
        dma((nz - 1,)),
        dma((3,)),
        dma((3,)),
        dma((chunks, 9)),
        dma((chunks, 9)),
    ]
    return pl.pallas_call(
        functools.partial(kernel, (nz, ny)),
        out_shape=jax.ShapeDtypeStruct((tok, chans), bf16),
        in_specs=[pl.BlockSpec(memory_space=pltpu.HBM)] * 8,
        out_specs=pl.BlockSpec(memory_space=pltpu.VMEM),
        scratch_shapes=scratch,
        compiler_params=pltpu.CompilerParams(
            collective_id=0, has_side_effects=True, vmem_limit_bytes=40 << 20
        ),
    )(
        *(
            pltpu.with_memory_space_constraint(array, pltpu.HBM)
            for array in (
                gate_input,
                key_input,
                value_input,
                decay_rate,
                frequency,
                residue,
                skip_gain.reshape(1, chans),
                out_weight,
            )
        )
    )


def solution(mesh):
    placed = (
        P("ctx", "ch"),
        P("ctx", "ch"),
        P("ctx", "ch"),
        P(None, "ch"),
        P(None, "ch"),
        P(None, None, "ch"),
        P("ch"),
        P("ctx", "ch"),
    )
    return jax.shard_map(
        on_device, mesh=mesh, in_specs=placed, out_specs=P("ctx", "ch"), check_vma=False
    )
```

```python
import functools

import jax
import jax.numpy as jnp
from jax import lax
from jax.experimental import pallas as pl
from jax.experimental.pallas import tpu as pltpu
from jax.sharding import PartitionSpec as P

MESH = pl.DeviceIdType.MESH
NX = 4
L = 16
NB = 8
CHUNKS = 4
PIECES = 2


def cmul(a_re, a_im, b_re, b_im):
    return (a_re * b_re - a_im * b_im, a_re * b_im + a_im * b_re)


def remote(src, dst, send_sem, recv_sem, device):
    return pltpu.make_async_remote_copy(
        src_ref=src,
        dst_ref=dst,
        send_sem=send_sem,
        recv_sem=recv_sem,
        device_id=device,
        device_id_type=MESH,
    )


def small_trig(angle):
    q = angle * angle
    cos = 1.0 + q * (-1.0 / 2 + q * (1.0 / 24 + q * (-1.0 / 720 + q * (1.0 / 40320))))
    sin = angle * (1.0 + q * (-1.0 / 6 + q * (1.0 / 120 + q * (-1.0 / 5040 + q * (1.0 / 362880)))))
    return cos, sin


def kernel(
    cfg,
    gate_h, key_h, value_h, decay_h, freq_h, residue_h, skip_h, weight_h,
    out,
    wfull, gall, gate, key, value, decay, freq, residue, skip,
    sig, near, acc,
    pow_re, pow_im, out_re, out_im, toep, hpad,
    ent_re, ent_im, beg_re, beg_im, cur_re, cur_im, co_re, co_im,
    esend, qpow, xin, zin, rsum, sx, sin,
    in_s, know, ax_s, ax_r, az_s, az_r, bz_s, bz_r, bx_s, bx_r,
    xo_s, xo_r, zo_s, zo_r, xb_s, xb_r, y_s, y_r,
):
    nz, ny = cfg
    tok, chans = key.shape
    modes = decay.shape[0]
    blocks = tok // L
    nb = min(NB, blocks)
    lanes = chans // NX
    rows = wfull.shape[1]
    ra = rows // 4
    steps = nz // 2
    zlim = ((1, steps), (-1, steps - 1))
    chunks = min(CHUNKS, blocks)
    chunk = tok // chunks
    per_chunk = blocks // chunks

    ctx = lax.axis_index("ctx")
    ch = lax.axis_index("ch")
    z, x = ctx // NX, lax.rem(ctx, NX)
    y, core = ch // 2, lax.rem(ch, 2)

    def wrap(value, size):
        value = jnp.where(value < 0, value + size, value)
        return jnp.where(value >= size, value - size, value)

    z_at = {d: (wrap(z + d, nz) * NX + x, ch) for d in range(1 - nz, nz)}
    x_of = {d: wrap(x + d, NX) for d in range(1 - NX, NX)}
    x_at = {d: (z * NX + x_of[d], ch) for d in x_of}
    y_of = {d: wrap(y + d, ny) * 2 + core for d in (-1, 0, 1, 2)}
    y_at = {d: (ctx, y_of[d]) for d in y_of}
    at_z, at_x, at_y = z_at.get, x_at.get, y_at.get
    other = (ctx, y * 2 + 1 - core)

    fetches = [
        pltpu.make_async_copy(src, dst, in_s.at[i])
        for i, (src, dst) in enumerate(
            (
                (decay_h, decay),
                (freq_h, freq),
                (key_h, key),
                (value_h, value),
                (weight_h, wfull.at[ctx]),
                (residue_h, residue),
                (skip_h, skip),
                (gate_h, gate),
            )
        )
    ]
    for fetch in fetches:
        fetch.start()
    for d in range(nz - 1):
        zin[d] = jnp.zeros(zin.shape[1:], zin.dtype)

    peers = [at_z(1), at_z(-1)] + [at_x(d) for d in range(1, NX)]
    if ny > 1:
        peers += [at_y(1), at_y(-1), at_y(2), other]
    barrier = pltpu.get_barrier_semaphore()
    for peer in peers:
        pl.semaphore_signal(barrier, inc=1, device_id=peer, device_id_type=MESH)

    fetches[4].wait()
    pl.semaphore_wait(barrier, len(peers))

    def a_first(d):
        part = wfull.at[ctx, 0:ra]
        return remote(part, part, ax_s.at[d - 1], ax_r.at[d - 1], at_x(d))

    def bz_step(dirn, k, sgn, src_z):
        part = wfull.at[src_z * NX + x, ra:rows]
        return remote(part, part, bz_s.at[dirn, k], bz_r.at[dirn, k], at_z(sgn))

    def bx_step(idx, src_z, d, from_x):
        part = wfull.at[src_z * NX + from_x, ra:rows]
        return remote(part, part, bx_s.at[idx, d - 1], bx_r.at[idx, d - 1], at_x(d))

    def origin(sgn, k):
        return wrap(z - sgn * k, nz)

    for dirn, (sgn, lim) in enumerate(zlim):
        bz_step(dirn, 1, sgn, z).start()
    for d in (2, 1, 3):
        a_first(d).start()
    for d in (2, 1, 3):
        bx_step(0, z, d, x).start()

    def w_event(j):
        for dirn, (sgn, lim) in enumerate(zlim):

            @pl.when(j <= lim)
            def _():
                src_z = origin(sgn, j)
                bz_step(dirn, j, sgn, src_z).wait_recv()

                @pl.when(j < lim)
                def _():
                    bz_step(dirn, j + 1, sgn, src_z).start()

                for d in (2, 1, 3):
                    bx_step(dirn * steps + j, src_z, d, x).start()

        @pl.when(j == 1)
        def _():
            for d in range(1, NX):
                a_first(d).wait_recv()
            for i in range(PIECES):
                for dirn, (sgn, lim) in enumerate(zlim):
                    a_next(dirn, 1, i, sgn, z).start()

        k = j - 1
        for i in range(PIECES):
            for dirn, (sgn, lim) in enumerate(zlim):

                @pl.when(jnp.logical_and(k >= 1, k <= lim))
                def _():
                    src_z = origin(sgn, k)
                    a_next(dirn, k, i, sgn, src_z).wait_recv()

                    @pl.when(k < lim)
                    def _():
                        a_next(dirn, k + 1, i, sgn, src_z).start()

    def a_next(dirn, k, i, sgn, src_z):
        part = wfull.at[pl.ds(src_z * NX + i * (NX // PIECES), NX // PIECES), 0:ra]
        return remote(part, part, az_s.at[dirn, k, i], az_r.at[dirn, k, i], at_z(sgn))

    def tell(r):
        for d in (1 << r, -(1 << r)):
            pl.semaphore_signal(know.at[r], inc=1, device_id=at_z(d), device_id_type=MESH)

    rounds = steps.bit_length() - 1

    def hear(r):
        if r < rounds:
            pl.semaphore_wait(know.at[r], 2)
            if r + 1 < rounds:
                tell(r + 1)

    tell(0)

    fetches[0].wait()
    fetches[1].wait()
    damp = 0.125 * decay[...]
    turn = 0.125 * freq[...]
    fade = jnp.exp(-damp)
    cos, sine = small_trig(turn)
    lam_re, lam_im = fade * cos, fade * sine
    power = (jnp.ones_like(lam_re), jnp.zeros_like(lam_im))
    for k in range(L + 1):
        pow_re[k] = power[0]
        pow_im[k] = power[1]
        power = cmul(power[0], power[1], lam_re, lam_im)

    fetches[2].wait()
    fetches[3].wait()

    def signals(i, _):
        at = pl.multiple_of(i * L, L)
        both = key[pl.ds(at, L), :].astype(jnp.float32) * value[pl.ds(at, L), :].astype(jnp.float32)
        for g in range(NX):
            sig[g, pl.ds(at, L), :] = both[:, g * lanes : (g + 1) * lanes]
        return 0

    lax.fori_loop(0, blocks, signals, 0, unroll=2)

    def lane_group(g):
        return pl.ds(pl.multiple_of(g * lanes, lanes), lanes)

    groups = blocks // nb

    def entries(i, _):
        g = i // groups
        at, first = lane_group(g), pl.multiple_of(lax.rem(i, groups) * nb * L, nb * L)
        totals = [[jnp.zeros((modes, lanes), jnp.float32)] * 2 for _ in range(nb)]
        for s in range(L):
            p_re, p_im = pow_re[L - 1 - s, :, at], pow_im[L - 1 - s, :, at]
            for b in range(nb):
                row = sig[g, pl.ds(first + (b * L + s), 1), :]
                totals[b] = [totals[b][0] + p_re * row, totals[b][1] + p_im * row]
        for b in range(nb):
            ent_re[lax.rem(i, groups) * nb + b, :, at] = totals[b][0]
            ent_im[lax.rem(i, groups) * nb + b, :, at] = totals[b][1]
        return 0

    lax.fori_loop(0, NX * groups // 2, entries, 0)
    hear(0)
    w_event(1)
    lax.fori_loop(NX * groups // 2, NX * groups, entries, 0)

    def advance(b, state):
        moved = cmul(*state, pow_re[L], pow_im[L])
        return (moved[0] + ent_re[b], moved[1] + ent_im[b])

    empty = jnp.zeros((modes, chans), jnp.float32)
    whole = lax.fori_loop(0, blocks, advance, (empty, empty))
    for q in range(NX):
        for part in range(2):
            esend[q, part] = whole[part][:, q * lanes : (q + 1) * lanes]

    def x_out(d):
        to = x_of[d]
        return remote(esend.at[to], xin.at[x], xo_s.at[d - 1], xo_r.at[d - 1], at_x(d))

    def z_out(d):
        return remote(rsum, zin.at[d - 1], zo_s.at[d - 1], zo_r.at[d - 1], at_z(d))

    def x_back(d):
        to = x_of[d]
        return remote(sx.at[to], sin.at[x], xb_s.at[d - 1], xb_r.at[d - 1], at_x(d))

    for d in (2, 1, 3):
        x_out(d).start()
    xin[x] = esend[x]
    hear(1)

    fade_q = jnp.exp(-damp * float(tok))
    q_re = fade_q * jnp.cos(turn * float(tok))
    q_im = fade_q * jnp.sin(turn * float(tok))
    for q in range(NX):
        qpow[q, 0] = q_re[:, q * lanes : (q + 1) * lanes]
        qpow[q, 1] = q_im[:, q * lanes : (q + 1) * lanes]
    for i in (5, 6, 7):
        fetches[i].wait()
    scale = jnp.sqrt(2.0 * damp)
    co_re[...] = scale * residue[0]
    co_im[...] = scale * residue[1]

    place = lax.broadcasted_iota(jnp.int32, (8, chans), 0)

    def out_tables(n, total):
        def row(ref, k):
            return jnp.broadcast_to(ref[k, pl.ds(n, 1), :], (8, chans))

        c_re = jnp.broadcast_to(co_re[pl.ds(n, 1), :], (8, chans))
        c_im = jnp.broadcast_to(co_im[pl.ds(n, 1), :], (8, chans))
        v = cmul(c_re, c_im, row(pow_re, 1), row(pow_im, 1))
        for bit in (1, 2, 4):
            w = cmul(*v, row(pow_re, bit), row(pow_im, bit))
            on = (place & bit) != 0
            v = (jnp.where(on, w[0], v[0]), jnp.where(on, w[1], v[1]))
        hi = cmul(*v, row(pow_re, 8), row(pow_im, 8))
        t_re = jnp.concatenate([v[0], hi[0]], axis=0)
        out_re[n] = t_re
        out_im[n] = jnp.concatenate([v[1], hi[1]], axis=0)
        return total + t_re

    def filters():
        later = lax.fori_loop(0, modes, out_tables, jnp.zeros((L, chans), jnp.float32))
        hpad[0:L, :] = jnp.zeros((L, chans), jnp.float32)
        hpad[L - 1 : L, :] = jnp.sum(co_re[...], axis=0, keepdims=True) + skip[...]
        hpad[L : 2 * L, :] = later
        for s in range(L):
            toep[s] = hpad[L - 1 - s : 2 * L - 1 - s, :]

    def near_part(i, _):
        g = i // groups
        at, first = lane_group(g), pl.multiple_of(lax.rem(i, groups) * nb * L, nb * L)
        totals = [jnp.zeros((L, lanes), jnp.float32) for _ in range(nb)]
        for s in range(L):
            table = toep[s, :, at]
            for b in range(nb):
                totals[b] = totals[b] + table * sig[g, pl.ds(first + (b * L + s), 1), :]
        for b in range(nb):
            near[pl.ds(pl.multiple_of(first + b * L, L), L), at] = totals[b]
        return 0

    def stage_row():
        for d in range(1, NX):
            x_out(d).wait_recv()
        one = (qpow[x, 0], qpow[x, 1])
        total = (xin[0, 0], xin[0, 1])
        for i in range(1, NX):
            moved = cmul(*total, *one)
            total = (moved[0] + xin[i, 0], moved[1] + xin[i, 1])
        rsum[0] = total[0].astype(rsum.dtype)
        rsum[1] = total[1].astype(rsum.dtype)
        hear(2)
        for d in sorted(range(1, nz), key=lambda d: -min(d, nz - d)):
            pl.when(z + d < nz)(z_out(d).start)

    def stage_z():
        one = (qpow[x, 0], qpow[x, 1])
        two = cmul(*one, *one)
        step = cmul(*two, *two)
        for d in range(1, nz):
            pl.when(z >= d)(z_out(d).wait_recv)
        total = (jnp.zeros((modes, lanes), jnp.float32),) * 2
        for d in range(nz - 1, 0, -1):
            moved = cmul(*total, *step)
            total = (
                moved[0] + zin[d - 1, 0].astype(jnp.float32),
                moved[1] + zin[d - 1, 1].astype(jnp.float32),
            )
        for i in range(NX):
            sx[i, 0] = total[0]
            sx[i, 1] = total[1]
            moved = cmul(*total, *one)
            total = (moved[0] + xin[i, 0], moved[1] + xin[i, 1])
        for d in (2, 1, 3):
            x_back(d).start()
        sin[x] = sx[x]

    def stage_begin():
        for d in range(1, NX):
            x_back(d).wait_recv()
        for q in range(NX):
            cur_re[:, q * lanes : (q + 1) * lanes] = sin[q, 0]
            cur_im[:, q * lanes : (q + 1) * lanes] = sin[q, 1]

    def far_chunk(c):
        state = (cur_re[...], cur_im[...])
        for i in range(per_chunk):
            for g in range(NX):
                beg_re[g, i] = state[0][:, g * lanes : (g + 1) * lanes]
                beg_im[g, i] = state[1][:, g * lanes : (g + 1) * lanes]
            moved = cmul(*state, pow_re[L], pow_im[L])
            b = c * per_chunk + i
            state = (moved[0] + ent_re[b], moved[1] + ent_im[b])
        cur_re[...] = state[0]
        cur_im[...] = state[1]

        def far_part(g, _):
            at = lane_group(g)
            spots = [pl.ds(pl.multiple_of(c * chunk + i * L, L), L) for i in range(per_chunk)]
            totals = [near[spot, at] for spot in spots]
            for n in range(modes):
                t_re, t_im = out_re[n, :, at], out_im[n, :, at]
                for i in range(per_chunk):
                    totals[i] = totals[i] + (
                        t_re * beg_re[g, i, n : n + 1, :] - t_im * beg_im[g, i, n : n + 1, :]
                    )
            for spot, total in zip(spots, totals):
                gated = gate[spot, at].astype(jnp.float32) * total
                gall[ch, spot, at] = gated.astype(jnp.bfloat16)
            return 0

        lax.fori_loop(0, NX, far_part, 0)

    direct = chunks // 2

    def y_copy(c, i, straight):
        def block(dy, dev, lo=0, hi=chunk):
            at = c * chunk + lo
            part = gall.at[y_of[dy], pl.ds(pl.multiple_of(at, hi - lo), hi - lo)]
            return remote(part, part, y_s.at[c, i], y_r.at[c, i], dev)

        mid = chunk // 2
        if i == 0:
            return block(0, other)
        if i == 1:
            return block(0, at_y(1))
        if i == 2:
            return block(0, at_y(-1))
        if i == 3:
            return block(0, at_y(2)) if straight else block(-1, at_y(1), 0, mid)
        if i == 4:
            return block(1, at_y(-1), mid, chunk)
        if i == 5:
            return block(-1, other)
        if i == 6:
            return block(1, other)
        if i == 7:
            return block(2, other) if straight else block(2, other, 0, mid)
        return block(2, other, mid, chunk)

    def y_forward(c):
        if ny > 1:
            for i in (1, 2):
                y_copy(c, i, c >= direct).wait_recv()
                if c < direct:
                    y_copy(c, 2 + i, False).start()
                y_copy(c, 4 + i, c >= direct).start()

    def y_last(c):
        if ny > 1:
            if c < direct:
                for i in (3, 4):
                    y_copy(c, i, False).wait_recv()
                    y_copy(c, 4 + i, False).start()
            else:
                part = gall.at[y_of[2], c * chunk : (c + 1) * chunk]
                remote(part, part, y_s.at[c, 3], y_r.at[c, 3], at_y(2)).wait_recv()
                y_copy(c, 7, True).start()

    def far_all():
        def one(c, _):
            far_chunk(c)
            if ny > 1:
                for i in (1, 2, 0):
                    y_copy(c, i, False).start()

                @pl.when(c >= direct)
                def _():
                    y_copy(c, 3, True).start()

            return 0

        lax.fori_loop(0, chunks, one, 0)

    def stage_1():
        stage_row()
        filters()

    def stage_2():
        lax.fori_loop(0, NX * groups, near_part, 0)

    def stage_5():
        stage_begin()
        far_all()

    def stage_6():
        y_forward(0)
        y_forward(1)

    def stage_7():
        if chunks > 2:
            y_forward(2)
            y_forward(3)
        y_last(0)

    def stage_8():
        for c in range(1, chunks):
            y_last(c)

    stages = (stage_1, stage_2, stage_z, stage_5, stage_6, stage_7, stage_8)

    def tick(k, _):
        pl.when(k <= steps + 1)(lambda: w_event(k))
        for i, stage in enumerate(stages):
            pl.when(k == i + 2)(stage)
        return 0

    lax.fori_loop(2, max(steps, len(stages)) + 2, tick, 0)

    def across(idx, _):
        off = jnp.where(idx <= steps, idx, steps - idx)
        for d in range(1, NX):
            bx_step(idx, wrap(z - off, nz), d, x_of[-d]).wait_recv()
        return 0

    lax.fori_loop(0, nz, across, 0)

    per = chans // rows

    def project(dy, side, first=False):
        if ny > 1:
            j = y_of[dy] + (0 if side == 0 else 1 - 2 * core)
        else:
            j = 0
        w = wfull[pl.ds(j * per, per)].reshape(chans, chans)
        term = jnp.dot(gall[j], w, preferred_element_type=jnp.float32)
        acc[...] = term if first else acc[...] + term

    project(0, 0, True)
    if ny > 1:
        project(-1, 0)
        project(1, 0)
        for dy, side, waits in ((0, 1, (0,)), (-1, 1, (5,)), (1, 1, (6,)), (2, 0, ()), (2, 1, (7, 8))):
            for c in range(chunks):
                for i in waits:
                    if i < 8 or c < direct:
                        y_copy(c, i, c >= direct).wait_recv()
            project(dy, side)
    out[...] = acc[...].astype(out.dtype)

    for d in range(1, NX):
        a_first(d).wait_send()
        x_out(d).wait_send()
        x_back(d).wait_send()
    for d in range(1, nz):
        pl.when(z + d < nz)(z_out(d).wait_send)

    def finish(k, _):
        for dirn, (sgn, lim) in enumerate(zlim):

            @pl.when(k <= lim)
            def _():
                src_z = origin(sgn, k - 1)
                bz_step(dirn, k, sgn, src_z).wait_send()
                for i in range(PIECES):
                    a_next(dirn, k, i, sgn, src_z).wait_send()

        return 0

    lax.fori_loop(1, steps + 1, finish, 0)

    def finish_x(idx, _):
        off = jnp.where(idx <= steps, idx, steps - idx)
        for d in range(1, NX):
            bx_step(idx, wrap(z - off, nz), d, x).wait_send()
        return 0

    lax.fori_loop(0, nz, finish_x, 0)
    if ny > 1:
        for c in range(chunks):
            for i in range(9):
                if c < direct or i not in (4, 8):
                    y_copy(c, i, c >= direct).wait_send()


def on_device(
    gate_input, key_input, value_input, decay_rate, frequency, residue, skip_gain, out_weight
):
    n_ctx, n_ch = lax.axis_size("ctx"), lax.axis_size("ch")
    nz, ny = n_ctx // NX, n_ch // 2
    tok, chans = key_input.shape
    rows = out_weight.shape[0]
    modes = decay_rate.shape[0]
    lanes = chans // NX
    blocks = tok // L
    chunks = min(CHUNKS, blocks)
    f32, bf16 = jnp.float32, jnp.bfloat16
    dma = pltpu.SemaphoreType.DMA
    steps = nz // 2
    state = (2, modes, lanes)
    table = pltpu.VMEM((L + 1, modes, chans), f32)
    panel = pltpu.VMEM((tok, chans), f32)
    single = pltpu.VMEM((modes, chans), f32)
    scratch = [
        pltpu.VMEM((n_ctx, rows, chans), bf16),
        pltpu.VMEM((n_ch, tok, chans), bf16),
        pltpu.VMEM((tok, chans), bf16),
        pltpu.VMEM((tok, chans), bf16),
        pltpu.VMEM((tok, chans), bf16),
        single,
        single,
        pltpu.VMEM((2, modes, chans), f32),
        pltpu.VMEM((1, chans), f32),
        pltpu.VMEM((NX, tok, lanes), f32),
        panel,
        panel,
        table,
        table,
        pltpu.VMEM((modes, L, chans), f32),
        pltpu.VMEM((modes, L, chans), f32),
        pltpu.VMEM((L, L, chans), f32),
        pltpu.VMEM((2 * L, chans), f32),
        pltpu.VMEM((blocks, modes, chans), f32),
        pltpu.VMEM((blocks, modes, chans), f32),
        pltpu.VMEM((NX, blocks // chunks, modes, lanes), f32),
        pltpu.VMEM((NX, blocks // chunks, modes, lanes), f32),
        single,
        single,
        single,
        single,
        pltpu.VMEM((NX,) + state, f32),
        pltpu.VMEM((NX,) + state, f32),
        pltpu.VMEM((NX,) + state, f32),
        pltpu.VMEM((nz - 1,) + state, bf16),
        pltpu.VMEM(state, bf16),
        pltpu.VMEM((NX,) + state, f32),
        pltpu.VMEM((NX,) + state, f32),
        dma((8,)),
        pltpu.SemaphoreType.REGULAR((4,)),
        dma((3,)),
        dma((3,)),
        dma((2, steps + 1, NX)),
        dma((2, steps + 1, NX)),
        dma((2, steps + 1)),
        dma((2, steps + 1)),
        dma((nz, 3)),
        dma((nz, 3)),
        dma((3,)),
        dma((3,)),
        dma((nz - 1,)),
        dma((nz - 1,)),
        dma((3,)),
        dma((3,)),
        dma((chunks, 9)),
        dma((chunks, 9)),
    ]
    return pl.pallas_call(
        functools.partial(kernel, (nz, ny)),
        out_shape=jax.ShapeDtypeStruct((tok, chans), bf16),
        in_specs=[pl.BlockSpec(memory_space=pltpu.HBM)] * 8,
        out_specs=pl.BlockSpec(memory_space=pltpu.VMEM),
        scratch_shapes=scratch,
        compiler_params=pltpu.CompilerParams(
            collective_id=0, has_side_effects=True, vmem_limit_bytes=40 << 20
        ),
    )(
        *(
            pltpu.with_memory_space_constraint(array, pltpu.HBM)
            for array in (
                gate_input,
                key_input,
                value_input,
                decay_rate,
                frequency,
                residue,
                skip_gain.reshape(1, chans),
                out_weight,
            )
        )
    )


def solution(mesh):
    placed = (
        P("ctx", "ch"),
        P("ctx", "ch"),
        P("ctx", "ch"),
        P(None, "ch"),
        P(None, "ch"),
        P(None, None, "ch"),
        P("ch"),
        P("ctx", "ch"),
    )
    return jax.shard_map(
        on_device, mesh=mesh, in_specs=placed, out_specs=P("ctx", "ch"), check_vma=False
    )
```
